32 devices in a mesh: row: 4 (over y, x), col: 8 (over z, core).
Axes of the slice: x: 2, y: 2, z: 4, core: 2. Of those that a mesh axis runs over, the one named last changes fastest.
Arguments:
- parent_front: bfloat16 [28672, 28672], P('row', 'col'), may hold values from -6 to 6
- child_update: bfloat16 [2, 14336, 14336], P(None, 'row', 'col'), may hold values from -6 to 6
- parent_test: bfloat16 [28672, 448], P('col'), may hold values from -0.03125 to 0.03125
- child_test: bfloat16 [2, 14336, 448], P(None, 'col'), may hold values from -0.046875 to 0.046875
- child_map: int32 [2, 112], replicated, may hold values from 0 to 223, as said below
Outputs:
- leaf_basis: bfloat16 [224, 128, 448], P('row', 'col')
- couplings: float32 [32, 448, 448], P('row', 'col')
The draws below stay inside these ranges and needn't reach their ends.
Inputs may be any that keep to these rules, and one draw needn't show every extreme that they name: `child_map`: for each child the entries rise strictly along its blocks, and entry j is at least j.
All inputs are finite; a program needn't handle non-finite values.
Results may differ from the reference program's by a relative error of at most 0.006.
Values may be sent and summed in bfloat16 or wider, within the bound.
A program may use at most 192 MiB of HBM per device.

```python
import math
import jax
import jax.numpy as jnp
from jax import lax

M = 14336
R = 448
LEAF = 896
BLOCK = 128
P_SIZE = 28672


def draw_child_map(key, part):
    blocks = M // BLOCK
    half = blocks // 2
    positions = jnp.arange(blocks, dtype=jnp.int32)
    first_key = jax.random.fold_in(key, 11)
    level = jax.random.randint(jax.random.fold_in(first_key, 1), (), 1, 4)
    draws = jax.random.randint(jax.random.fold_in(first_key, 2), (blocks,), 0, 4)
    steps_up = (draws < level).astype(jnp.int32)
    first = positions + jnp.cumsum(steps_up).astype(jnp.int32)
    second_key = jax.random.fold_in(key, 12)
    gaps = jax.random.randint(jax.random.fold_in(second_key, 2), (blocks,), 0, 2)
    gaps = jnp.where(positions < half, gaps, 0).astype(jnp.int32)
    later = jnp.cumsum(gaps[::-1])[::-1].astype(jnp.int32) - gaps
    second = positions + blocks - later
    return jnp.stack([first, second]).astype(jnp.int32)


def level_of(own_key, dims, split, low, high):
    factor_of = 1.0
    for axis_at, blocks in split:
        heights = jax.random.uniform(jax.random.fold_in(jax.random.fold_in(own_key, 6), axis_at), (blocks,), jnp.float32, low / len(split), high / len(split))
        factor_of = factor_of * jnp.repeat(jnp.exp(heights), dims[axis_at] // blocks).reshape((-1,) + (1,) * (len(dims) - 1 - axis_at))
    return factor_of


def scatter_about(key, extent, spread, most, pieces=(), kind=jnp.bfloat16):
    drawn = jax.random.normal(key, extent, jnp.float32) * spread
    if len(pieces) > 0:
        drawn = level_of(key, extent, pieces, -0.22, 0.18) * drawn
    return jnp.clip(drawn, min=-most, max=most).astype(kind)


def setup_inputs(seed: int = 0) -> dict:
    keys = jax.random.split(jax.random.key(seed), 6)
    parent_front = scatter_about(keys[0], (P_SIZE, P_SIZE), 1.0, 6.0, ((0, 4), (1, 8)))
    child_update = scatter_about(keys[1], (2, M, M), 1.0, 6.0, ((1, 4), (2, 8)))
    parent_test = scatter_about(keys[2], (P_SIZE, R), P_SIZE ** -0.5, 0.03125, ((0, 8),))
    child_test = scatter_about(keys[3], (2, M, R), M ** -0.5, 0.046875, ((1, 8),))
    child_map = draw_child_map(jax.random.fold_in(keys[5], 71), 0)
    return {"parent_front": parent_front, "child_update": child_update, "parent_test": parent_test, "child_test": child_test, "child_map": child_map}


HIGH = lax.Precision.HIGHEST

def orthonormal(leaves):
    gram_matrix = jnp.einsum('lkr,lks->lrs', leaves, leaves, precision=HIGH)
    factor = jnp.linalg.cholesky(gram_matrix)
    solved = lax.linalg.triangular_solve(factor, leaves, left_side=False, lower=True, transpose_a=True)
    return (solved * math.sqrt(LEAF)).astype(jnp.bfloat16)

def reference(parent_front, child_update, parent_test, child_test, child_map):
    sample = jnp.dot(parent_front.astype(jnp.float32), parent_test.astype(jnp.float32), preferred_element_type=jnp.float32)
    sample = sample.reshape(2 * M // BLOCK, BLOCK, R)
    for which in range(2):
        probed = jnp.dot(child_update[which].astype(jnp.float32), child_test[which].astype(jnp.float32), preferred_element_type=jnp.float32)
        sample = sample.at[child_map[which]].add(probed.reshape(M // BLOCK, BLOCK, R))
    leaves = sample.reshape(2 * M // LEAF, LEAF, R)
    bases = orthonormal(leaves)
    shrink = 1.0 / math.sqrt(LEAF)

    def coupling(leaf_index):
        sibling = jnp.bitwise_xor(leaf_index, 1)
        front_tile = lax.dynamic_slice(parent_front, (leaf_index * LEAF, sibling * LEAF), (LEAF, LEAF))
        product = (jnp.dot(front_tile.astype(jnp.float32), bases[sibling].astype(jnp.float32), preferred_element_type=jnp.float32) * shrink).astype(jnp.bfloat16)
        return jnp.dot(bases[leaf_index].T.astype(jnp.float32), product.astype(jnp.float32), preferred_element_type=jnp.float32) * shrink
    couplings = lax.map(coupling, jnp.arange(2 * M // LEAF, dtype=jnp.int32))
    return (bases.reshape(2 * M // BLOCK, BLOCK, R), couplings)
```

```python
import functools
import math

import jax
import jax.numpy as jnp
from jax import lax
from jax.experimental import pallas as pl
from jax.experimental.pallas import tpu as pltpu
from jax.sharding import PartitionSpec as P

LEAF = 896
BLOCK = 128
PIVOTS = 64
GROUP = 4

HIGH = lax.Precision.HIGHEST


def dot(a, b, dims):
    return lax.dot_general(
        a, b, (dims, ((), ())), precision=HIGH, preferred_element_type=jnp.float32
    )


def inverse_factor(tile, nb):
    ridx = lax.broadcasted_iota(jnp.int32, tile.shape, 0)
    lane = lax.broadcasted_iota(jnp.int32, tile.shape, 1)
    for j in range(0, nb, GROUP):
        cols = [
            jnp.broadcast_to(tile[:, nb + j + k : nb + j + k + 1], tile.shape)
            for k in range(GROUP)
        ]
        rows = [tile[j + k : j + k + 1, :] for k in range(GROUP)]
        for k in range(GROUP):
            at = j + k
            factor = jnp.where(ridx > at, cols[k] * (1.0 / cols[k][at : at + 1, :]), 0.0)
            for m in range(k + 1, GROUP):
                cols[m] = cols[m] - factor * cols[m][at : at + 1, :]
                rows[m] = rows[m] - factor[j + m : j + m + 1, :] * rows[k]
            cols[k] = factor
        for k in range(GROUP):
            tile = tile - cols[k] * rows[k]
    pivots = jnp.sum(jnp.where(lane == ridx + nb, tile, 0.0), axis=1, keepdims=True)
    return tile[:, :nb] * lax.rsqrt(pivots)


def basis_kernel(scale, yt_ref, qt_ref, gram_ref, work_ref):
    nb = PIVOTS
    probes = yt_ref.shape[0]
    work_ref[...] = yt_ref[...]
    gram_ref[...] = dot(yt_ref[...], yt_ref[...], ((1,), (1,)))

    def step(index, carry):
        start = pl.multiple_of(index * nb, nb)
        panel = gram_ref[pl.ds(start, nb), :]
        source = lax.broadcasted_iota(jnp.int32, (probes, 2 * nb), 0)
        lane = lax.broadcasted_iota(jnp.int32, (probes, 2 * nb), 1)
        pick = jnp.where((lane >= nb) & (source == lane - nb + start), 1.0, 0.0)
        eye = jnp.where(
            lax.broadcasted_iota(jnp.int32, (nb, 2 * nb), 0)
            == lax.broadcasted_iota(jnp.int32, (nb, 2 * nb), 1),
            1.0,
            0.0,
        )
        inverse = inverse_factor(dot(panel, pick, ((1,), (0,))) + eye, nb)
        top = dot(inverse, panel, ((1,), (0,)))
        solved = dot(inverse, work_ref[pl.ds(start, nb), :], ((1,), (0,)))
        qt_ref[pl.ds(start, nb), :] = (solved * scale).astype(qt_ref.dtype)
        gram_ref[...] -= dot(top, top, ((0,), (0,)))
        work_ref[...] -= dot(top, solved, ((0,), (0,)))
        return carry

    lax.fori_loop(0, probes // nb, step, 0)


def leaf_basis_of(yt):
    probes, rows = yt.shape
    return pl.pallas_call(
        functools.partial(basis_kernel, math.sqrt(LEAF)),
        out_shape=jax.ShapeDtypeStruct((probes, rows), jnp.bfloat16),
        in_specs=[pl.BlockSpec(memory_space=pltpu.VMEM)],
        out_specs=pl.BlockSpec(memory_space=pltpu.VMEM),
        scratch_shapes=[
            pltpu.VMEM((probes, probes), jnp.float32),
            pltpu.VMEM((probes, rows), jnp.float32),
        ],
        compiler_params=pltpu.CompilerParams(vmem_limit_bytes=40 << 20),
        cost_estimate=pl.CostEstimate(
            flops=40 * probes * probes * rows,
            bytes_accessed=6 * probes * rows,
            transcendentals=0,
        ),
        name="leaf_basis",
    )(yt)


def reduce_slabs(partial, col_count, col_index):
    blocks = partial.shape[0] // BLOCK
    slab = BLOCK // col_count
    pairs = col_count // 2
    probes = partial.shape[1]
    pair_index = col_index // 2
    parity = col_index % 2
    view = partial.reshape(blocks, pairs, 2, slab, probes)
    swapped = lax.ppermute(
        lax.dynamic_index_in_dim(view, 1 - parity, 2, False),
        "col",
        [(c, c ^ 1) for c in range(col_count)],
    )
    kept = lax.dynamic_index_in_dim(view, parity, 2, False)

    def piece(pair):
        return lax.dynamic_index_in_dim(kept, pair, 1, False) + lax.dynamic_index_in_dim(
            swapped, pair, 1, False
        )

    total = piece(pair_index)
    for shift in range(1, pairs):
        sent = piece((pair_index + shift) % pairs).astype(jnp.bfloat16)
        came = lax.ppermute(
            sent, "col", [(c, (c + 2 * shift) % col_count) for c in range(col_count)]
        )
        total = total + came.astype(jnp.float32)
    return total


def local(parent_front, child_update, parent_test, child_test, child_map):
    row_count = lax.axis_size("row")
    col_count = lax.axis_size("col")
    row_index = lax.axis_index("row")
    col_index = lax.axis_index("col")
    slab = BLOCK // col_count
    own_blocks = parent_front.shape[0] // BLOCK
    kid_blocks = child_update.shape[1] // BLOCK
    probes = parent_test.shape[1]
    per_leaf = LEAF // BLOCK
    leaf_count = own_blocks // per_leaf
    col_leaves = parent_front.shape[1] // LEAF
    shrink = 1.0 / math.sqrt(LEAF)

    kid_probe = jnp.einsum(
        "cmk,ckr->cmr", child_update, child_test, preferred_element_type=jnp.float32
    )
    kid_share = reduce_slabs(
        kid_probe.reshape(2 * kid_blocks * BLOCK, probes), col_count, col_index
    ).reshape(2, kid_blocks, slab, probes)
    all_kids = lax.all_gather(kid_share, "row", axis=1, tiled=True)

    own_probe = jnp.dot(parent_front, parent_test, preferred_element_type=jnp.float32)
    own_share = reduce_slabs(own_probe, col_count, col_index)

    targets = jnp.arange(own_blocks, dtype=jnp.int32)
    mapped = child_map - row_index * own_blocks
    onehot = (mapped[:, None, :] == targets[None, :, None]).astype(jnp.float32)
    sample = own_share + jnp.einsum("cpn,cnsr->psr", onehot, all_kids, precision=HIGH)

    by_leaf = sample.reshape(leaf_count, per_leaf * slab, probes)
    by_leaf = jnp.pad(by_leaf, ((0, col_count - leaf_count), (0, 0), (0, 0)))
    leaf_rows = lax.all_to_all(by_leaf, "col", 0, 0, tiled=True).reshape(LEAF, probes)

    front = parent_front
    pieces = []
    for position in range(col_leaves):
        sibling = col_index * col_leaves + position
        row_start = jnp.bitwise_xor(sibling, 1) % leaf_count * LEAF
        tile = lax.dynamic_slice(front, (row_start, position * LEAF), (LEAF, LEAF))
        routes = []
        for row in range(row_count):
            for slot in range(leaf_count):
                other = (row * leaf_count + slot) ^ 1
                if other % col_leaves == position:
                    routes.append(
                        (row * col_count + other // col_leaves, row * col_count + slot)
                    )
        pieces.append(lax.ppermute(tile, ("row", "col"), routes))
    wanted = jnp.bitwise_xor(col_index, 1) % col_leaves
    front_tile = pieces[0]
    for position in range(1, col_leaves):
        front_tile = jnp.where(wanted == position, pieces[position], front_tile)

    basis_t = leaf_basis_of(leaf_rows.T)
    basis = basis_t.T
    slabs = lax.all_to_all(
        basis.reshape(col_count, per_leaf * slab, probes), "col", 0, 0, tiled=True
    )
    leaf_basis = slabs[:leaf_count].reshape(own_blocks, slab, probes)

    natural = (
        basis.reshape(col_count, per_leaf, slab, probes)
        .transpose(1, 0, 2, 3)
        .reshape(LEAF, probes)
    )
    sibling_basis = lax.ppermute(natural, "col", [(c, c ^ 1) for c in range(col_count)])
    product = jnp.dot(front_tile, sibling_basis, preferred_element_type=jnp.float32) * shrink
    core = (
        lax.dot_general(
            natural,
            product.astype(jnp.bfloat16),
            (((0,), (0,)), ((), ())),
            preferred_element_type=jnp.float32,
        )
        * shrink
    )
    cores = lax.all_to_all(
        core.reshape(col_count, probes // col_count, probes), "col", 0, 0, tiled=True
    )
    return (leaf_basis, cores[:leaf_count])


def solution(mesh):
    in_specs = (P("row", "col"), P(None, "row", "col"), P("col", None), P(None, "col", None), P())
    out_specs = (P("row", "col", None), P("row", "col", None))
    return jax.shard_map(local, mesh=mesh, in_specs=in_specs, out_specs=out_specs, check_vma=False)
```

```python
import functools
import math

import jax
import jax.numpy as jnp
from jax import lax
from jax.experimental import pallas as pl
from jax.experimental.pallas import tpu as pltpu
from jax.sharding import PartitionSpec as P


LEAF = 896
BLOCK = 128
PIVOTS = 64
GROUP = 4

HIGH = lax.Precision.HIGHEST


def dot(a, b, dims):
    return lax.dot_general(
        a, b, (dims, ((), ())), precision=HIGH, preferred_element_type=jnp.float32
    )


def inverse_factor(tile, nb):
    ridx = lax.broadcasted_iota(jnp.int32, tile.shape, 0)
    lane = lax.broadcasted_iota(jnp.int32, tile.shape, 1)
    for j in range(0, nb, GROUP):
        cols = [
            jnp.broadcast_to(tile[:, nb + j + k : nb + j + k + 1], tile.shape)
            for k in range(GROUP)
        ]
        rows = [tile[j + k : j + k + 1, :] for k in range(GROUP)]
        for k in range(GROUP):
            at = j + k
            factor = jnp.where(ridx > at, cols[k] * (1.0 / cols[k][at : at + 1, :]), 0.0)
            for m in range(k + 1, GROUP):
                cols[m] = cols[m] - factor * cols[m][at : at + 1, :]
                rows[m] = rows[m] - factor[j + m : j + m + 1, :] * rows[k]
            cols[k] = factor
        for k in range(GROUP):
            tile = tile - cols[k] * rows[k]
    pivots = jnp.sum(jnp.where(lane == ridx + nb, tile, 0.0), axis=1, keepdims=True)
    return tile[:, :nb] * lax.rsqrt(pivots)


def basis_kernel(scale, yt_ref, qt_ref, gram_ref, work_ref):
    nb = PIVOTS
    probes = yt_ref.shape[0]
    work_ref[...] = yt_ref[...]
    gram_ref[...] = dot(yt_ref[...], yt_ref[...], ((1,), (1,)))

    def step(index, carry):
        start = pl.multiple_of(index * nb, nb)
        panel = gram_ref[pl.ds(start, nb), :]
        source = lax.broadcasted_iota(jnp.int32, (probes, 2 * nb), 0)
        lane = lax.broadcasted_iota(jnp.int32, (probes, 2 * nb), 1)
        pick = jnp.where((lane >= nb) & (source == lane - nb + start), 1.0, 0.0)
        eye = jnp.where(
            lax.broadcasted_iota(jnp.int32, (nb, 2 * nb), 0)
            == lax.broadcasted_iota(jnp.int32, (nb, 2 * nb), 1),
            1.0,
            0.0,
        )
        inverse = inverse_factor(dot(panel, pick, ((1,), (0,))) + eye, nb)
        top = dot(inverse, panel, ((1,), (0,)))
        solved = dot(inverse, work_ref[pl.ds(start, nb), :], ((1,), (0,)))
        qt_ref[pl.ds(start, nb), :] = (solved * scale).astype(qt_ref.dtype)
        gram_ref[...] -= dot(top, top, ((0,), (0,)))
        work_ref[...] -= dot(top, solved, ((0,), (0,)))
        return carry

    lax.fori_loop(0, probes // nb, step, 0)


def leaf_basis_of(yt):
    probes, rows = yt.shape
    return pl.pallas_call(
        functools.partial(basis_kernel, math.sqrt(LEAF)),
        out_shape=jax.ShapeDtypeStruct((probes, rows), jnp.bfloat16),
        in_specs=[pl.BlockSpec(memory_space=pltpu.VMEM)],
        out_specs=pl.BlockSpec(memory_space=pltpu.VMEM),
        scratch_shapes=[
            pltpu.VMEM((probes, probes), jnp.float32),
            pltpu.VMEM((probes, rows), jnp.float32),
        ],
        compiler_params=pltpu.CompilerParams(vmem_limit_bytes=40 << 20),
        cost_estimate=pl.CostEstimate(
            flops=40 * probes * probes * rows,
            bytes_accessed=6 * probes * rows,
            transcendentals=0,
        ),
        name="leaf_basis",
    )(yt)


def probe_kernel(parity_ref, front_ref, test_ref, kept_ref, sent_ref):
    total = jnp.dot(front_ref[...], test_ref[...], preferred_element_type=jnp.float32)
    blocks, pairs, slab, probes = kept_ref.shape
    view = total.reshape(blocks * pairs, 2, slab, probes)
    even = parity_ref[0] == 0
    kept_ref[...] = jnp.where(even, view[:, 0], view[:, 1]).reshape(kept_ref.shape)
    sent_ref[...] = jnp.where(even, view[:, 1], view[:, 0]).reshape(sent_ref.shape)


def probe(front, test, which, first_row, rows, col_count, parity):
    depth, probes = test.shape[1:]
    tile = max(t for t in range(BLOCK, 4 * BLOCK + 1, BLOCK) if rows % t == 0)
    pairs, slab = col_count // 2, BLOCK // col_count
    half = jax.ShapeDtypeStruct((rows // BLOCK, pairs, slab, probes), jnp.float32)
    out_spec = pl.BlockSpec((tile // BLOCK, pairs, slab, probes), lambda i, p: (i, 0, 0, 0))
    skip = first_row // tile
    return pl.pallas_call(
        probe_kernel,
        out_shape=(half, half),
        grid_spec=pltpu.PrefetchScalarGridSpec(
            num_scalar_prefetch=1,
            grid=(rows // tile,),
            in_specs=[
                pl.BlockSpec((None, tile, depth), lambda i, p: (which, skip + i, 0)),
                pl.BlockSpec((None, depth, probes), lambda i, p: (which, 0, 0)),
            ],
            out_specs=(out_spec, out_spec),
        ),
        compiler_params=pltpu.CompilerParams(vmem_limit_bytes=40 << 20),
        cost_estimate=pl.CostEstimate(
            flops=2 * rows * depth * probes,
            bytes_accessed=2 * rows * depth + 2 * depth * probes + 4 * rows * probes,
            transcendentals=0,
        ),
        name="probe",
    )(parity, front, test)


def swap_pair(halves, col_count):
    kept, sent = halves
    return kept, lax.ppermute(sent, "col", [(c, c ^ 1) for c in range(col_count)])


def send_pairs(kept, swapped, col_count, pair_index):
    pairs = col_count // 2

    def piece(pair):
        return lax.dynamic_index_in_dim(kept, pair, 1, False) + lax.dynamic_index_in_dim(
            swapped, pair, 1, False
        )

    came = [
        lax.ppermute(
            piece((pair_index + shift) % pairs).astype(jnp.bfloat16),
            "col",
            [(c, (c + 2 * shift) % col_count) for c in range(col_count)],
        )
        for shift in range(1, pairs)
    ]
    return piece(pair_index), came


def add_up(own, came):
    for term in came:
        own = own + term.astype(jnp.float32)
    return own


def local(parent_front, child_update, parent_test, child_test, child_map):
    row_count = lax.axis_size("row")
    col_count = lax.axis_size("col")
    row_index = lax.axis_index("row")
    col_index = lax.axis_index("col")
    slab = BLOCK // col_count
    own_blocks = parent_front.shape[0] // BLOCK
    probes = parent_test.shape[1]
    per_leaf = LEAF // BLOCK
    leaf_count = own_blocks // per_leaf
    col_leaves = parent_front.shape[1] // LEAF
    shrink = 1.0 / math.sqrt(LEAF)

    tie = lax.optimization_barrier
    pair_index = col_index // 2
    parity = col_index % 2
    half = own_blocks // 2 * BLOCK
    sign = jnp.reshape(parity, (1,)).astype(jnp.int32)
    fronts, tests = parent_front[None], parent_test[None]
    kid_rows = child_update.shape[1]

    def send_tile(position, front):
        sibling = col_index * col_leaves + position
        row_start = jnp.bitwise_xor(sibling, 1) % leaf_count * LEAF
        tile = lax.dynamic_slice(front, (row_start, position * LEAF), (LEAF, LEAF))
        routes = []
        for row in range(row_count):
            for slot in range(leaf_count):
                other = (row * leaf_count + slot) ^ 1
                if other % col_leaves == position:
                    routes.append(
                        (row * col_count + other // col_leaves, row * col_count + slot)
                    )
        return lax.ppermute(tile, ("row", "col"), routes)

    pieces = {position: send_tile(position, parent_front) for position in range(0, col_leaves, 2)}

    jobs = (
        (child_update, child_test, 0, 0, kid_rows),
        (child_update, child_test, 1, 0, kid_rows),
        (fronts, tests, 0, 0, half),
        (fronts, tests, 0, half, half),
    )
    sums = []
    for front, test, which, first_row, rows in jobs:
        halves = probe(front, test, which, first_row, rows, col_count, sign)
        kept, swapped = swap_pair(halves, col_count)
        sums.append(send_pairs(kept, swapped, col_count, pair_index))
    (first_own, first_came), (second_own, second_came) = sums[:2]
    (upper_own, upper_came), (lower_own, lower_came) = sums[2:]

    kid_share = jnp.stack([add_up(first_own, first_came), add_up(second_own, second_came)])
    all_kids = lax.all_gather(kid_share, "row", axis=1, tiled=True)
    own_share = jnp.concatenate([add_up(upper_own, upper_came), add_up(lower_own, lower_came)])

    targets = jnp.arange(own_blocks, dtype=jnp.int32)
    mapped = child_map - row_index * own_blocks
    onehot = (mapped[:, None, :] == targets[None, :, None]).astype(jnp.float32)
    sample = own_share + jnp.einsum("cpn,cnsr->psr", onehot, all_kids, precision=HIGH)

    by_leaf = sample.reshape(leaf_count, per_leaf * slab, probes)
    by_leaf = jnp.pad(by_leaf, ((0, col_count - leaf_count), (0, 0), (0, 0)))
    leaf_rows = lax.all_to_all(by_leaf, "col", 0, 0, tiled=True).reshape(LEAF, probes)

    leaf_rows, front = tie((leaf_rows, parent_front))
    for position in range(1, col_leaves, 2):
        pieces[position] = send_tile(position, front)
    wanted = jnp.bitwise_xor(col_index, 1) % col_leaves
    front_tile = pieces[0]
    for position in range(1, col_leaves):
        front_tile = jnp.where(wanted == position, pieces[position], front_tile)

    basis_t = leaf_basis_of(leaf_rows.T)
    basis = basis_t.T
    slabs = lax.all_to_all(
        basis.reshape(col_count, per_leaf * slab, probes), "col", 0, 0, tiled=True
    )
    leaf_basis = slabs[:leaf_count].reshape(own_blocks, slab, probes)

    natural = (
        basis.reshape(col_count, per_leaf, slab, probes)
        .transpose(1, 0, 2, 3)
        .reshape(LEAF, probes)
    )
    sibling_basis = lax.ppermute(natural, "col", [(c, c ^ 1) for c in range(col_count)])
    product = jnp.dot(front_tile, sibling_basis, preferred_element_type=jnp.float32) * shrink
    core = (
        lax.dot_general(
            natural,
            product.astype(jnp.bfloat16),
            (((0,), (0,)), ((), ())),
            preferred_element_type=jnp.float32,
        )
        * shrink
    )
    cores = lax.all_to_all(
        core.reshape(col_count, probes // col_count, probes), "col", 0, 0, tiled=True
    )
    return (leaf_basis, cores[:leaf_count])


def solution(mesh):
    in_specs = (P("row", "col"), P(None, "row", "col"), P("col", None), P(None, "col", None), P())
    out_specs = (P("row", "col", None), P("row", "col", None))
    return jax.shard_map(local, mesh=mesh, in_specs=in_specs, out_specs=out_specs, check_vma=False)
```
